512 devices in a mesh: dp: 16 (over y, x), tensor: 32 (over z, core).
Axes of the slice: x: 4, y: 4, z: 16, core: 2. Of those that a mesh axis runs over, the one named last changes fastest.
Arguments:
- inputs: bfloat16 [2048, 4096], P('dp', 'tensor'), may hold values from -6 to 6
- cotangent: bfloat16 [2048, 4096], P('dp', 'tensor'), may hold values from -6 to 6
- gate_w: bfloat16 [32, 24, 128, 128], P('tensor'), may hold values from -0.25 to 0.25
- up_w: bfloat16 [32, 24, 128, 128], P('tensor'), may hold values from -0.25 to 0.25
- down_w: bfloat16 [32, 24, 128, 128], P('tensor'), may hold values from -0.25 to 0.25
- gate_list: int32 [32, 24], P('tensor'), may hold values from -1 to 127, as said below
- up_list: int32 [32, 24], P('tensor'), may hold values from -1 to 127, as said below
- down_list: int32 [32, 24], P('tensor'), may hold values from -1 to 127, as said below
Outputs:
- grad_x: bfloat16 [2048, 4096], P('dp', 'tensor')
- grad_gate_w: bfloat16 [32, 24, 128, 128], P('tensor', None, 'dp')
- grad_up_w: bfloat16 [32, 24, 128, 128], P('tensor', None, 'dp')
- grad_down_w: bfloat16 [32, 24, 128, 128], P('tensor', None, 'dp')
The draws below stay inside these ranges and needn't reach their ends.
Inputs may be any that keep to these rules, and one draw needn't show every extreme that they name: `gate_list`: row j of the list names blocks of hidden blocks j * 4 to j * 4 + 3 only; no entry appears twice in a row; live entries come first and -1 fills the rest; a row holds at most 24 live entries and some row holds exactly 24. `up_list`: as for gate_list, drawn independently. `down_list`: as for gate_list, drawn independently.
All inputs are finite; a program needn't handle non-finite values.
Results may differ from the reference program's by a relative error of at most 0.014.
Values may be sent and summed in bfloat16 or wider, within the bound.
No kernel may reach another device: no remote copies, remote signals or barrier semaphores. Data moves between devices by JAX's collectives and lax.ppermute only.
A program may use at most 64 MiB of HBM per device.

```python
import math
import jax
import jax.numpy as jnp
from jax import lax

D = 4096
BLOCK = 128
TOK = 128
HB = 4
DB = 32
NBLK = 24
TOKENS = 2048
N_DP = 16
N_TENSOR = 32


def make_list(key, salt):
    key = jax.random.fold_in(key, salt)
    key_count, key_top, key_pick = jax.random.split(key, 3)
    counts = jax.random.randint(key_count, (N_TENSOR,), NBLK // 3, NBLK + 1)
    chosen = jax.random.randint(key_top, (), 0, N_TENSOR)
    counts = jnp.where(jnp.arange(N_TENSOR) == chosen, NBLK, counts)
    slots = jnp.arange(NBLK)
    filler = HB * DB

    def pick_row(subkey, row_total):
        picked = jax.random.permutation(subkey, HB * DB)[:NBLK]
        kept = jnp.where(slots < row_total, picked, filler)
        ordered = jnp.sort(kept)
        return jnp.where(ordered == filler, -1, ordered)
    rows_all = jax.vmap(pick_row)(jax.random.split(key_pick, N_TENSOR), counts)
    return rows_all.astype(jnp.int32)


def draw_gate_list(key, part):
    return make_list(key, 11)


def draw_up_list(key, part):
    return make_list(key, 23)


def draw_down_list(key, part):
    return make_list(key, 37)


def shard_levels(key, dims, cuts, smallest, high):
    gain, own = 1.0, jax.random.fold_in(key, 6)
    for axis_at, parts in cuts:
        heights = jnp.exp(jax.random.uniform(jax.random.fold_in(own, axis_at), (parts,), jnp.float32, smallest / len(cuts), high / len(cuts)))
        gain = gain * jnp.repeat(heights, dims[axis_at] // parts).reshape([-1 if axis == axis_at else 1 for axis in range(len(dims))])
    return gain


def normal_values(own_key, shape, width, most, cuts=(), kind=jnp.bfloat16):
    loudness = shard_levels(own_key, shape, cuts, -0.22, 0.18) if cuts else 1.0
    result = jax.random.normal(own_key, shape, jnp.float32) * width * loudness
    return jnp.minimum(jnp.maximum(result, -most), most).astype(kind)


def setup_inputs(seed: int = 0) -> dict:
    streams_of = jax.random.split(jax.random.key(seed), 9)
    inputs = normal_values(streams_of[0], (TOKENS, D), 1.0, 6.0, ((0, 16), (1, 32)))
    cotangent = normal_values(streams_of[1], (TOKENS, D), 1.0, 6.0, ((0, 16), (1, 32)))
    gate_w = normal_values(streams_of[2], (N_TENSOR, NBLK, BLOCK, BLOCK), (D // 8) ** -0.5, 0.25, ((0, 32),))
    up_w = normal_values(streams_of[3], (N_TENSOR, NBLK, BLOCK, BLOCK), (D // 8) ** -0.5, 0.25, ((0, 32),))
    down_w = normal_values(streams_of[4], (N_TENSOR, NBLK, BLOCK, BLOCK), (D // 8) ** -0.5, 0.25, ((0, 32),))
    gate_list = draw_gate_list(jax.random.fold_in(streams_of[8], 71), 0)
    up_list = draw_up_list(jax.random.fold_in(streams_of[8], 71), 0)
    down_list = draw_down_list(jax.random.fold_in(streams_of[8], 71), 0)
    return {"inputs": inputs, "cotangent": cotangent, "gate_w": gate_w, "up_w": up_w, "down_w": down_w, "gate_list": gate_list, "up_list": up_list, "down_list": down_list}


def decode(entries, row_count):
    living = entries >= 0
    clamped = jnp.maximum(entries, 0)
    return (living, clamped // row_count, clamped % row_count)

def one_hot(block_index, width_count, living):
    return ((block_index[:, None] == jnp.arange(width_count)[None, :]) & living[:, None]).astype(jnp.float32)

def weight_term(products, grad_scale, living):
    rounded = (products * grad_scale).astype(jnp.bfloat16)
    rounded = lax.optimization_barrier(rounded)
    summed = lax.optimization_barrier(jnp.sum(rounded.astype(jnp.float32), axis=0))
    return (summed * living[:, None, None].astype(jnp.float32)).astype(jnp.bfloat16)

def reference(inputs, cotangent, gate_w, up_w, down_w, gate_list, up_list, down_list):
    highest = lax.Precision.HIGHEST
    grad_scale = 1.0 / math.sqrt(TOKENS)
    input_blocks = inputs.reshape(N_DP, TOK, DB, BLOCK)
    cot_blocks = cotangent.reshape(N_DP, TOK, DB, BLOCK)

    def owner(running, pieces):
        gate_blk, up_blk, down_blk, gate_ent, up_ent, down_ent = pieces
        gate_live, gate_feat, gate_row = decode(gate_ent, HB)
        up_live, up_feat, up_row = decode(up_ent, HB)
        down_live, down_feat, down_row = decode(down_ent, HB)
        gate_in = jnp.take(input_blocks, gate_feat, axis=2).astype(jnp.float32)
        up_in = jnp.take(input_blocks, up_feat, axis=2).astype(jnp.float32)
        gate_part = jnp.einsum('ptkc,kch->ptkh', gate_in, gate_blk.astype(jnp.float32))
        gate_val = jnp.einsum('ptkh,kr->ptrh', gate_part, one_hot(gate_row, HB, gate_live), precision=highest)
        up_part = jnp.einsum('ptkc,kch->ptkh', up_in, up_blk.astype(jnp.float32))
        up_val = jnp.einsum('ptkh,kr->ptrh', up_part, one_hot(up_row, HB, up_live), precision=highest)
        sigmoid_gate = jax.nn.sigmoid(gate_val)
        active = gate_val * sigmoid_gate
        hidden = (active * up_val).astype(jnp.bfloat16)
        down_cot = jnp.take(cot_blocks, down_feat, axis=2).astype(jnp.float32)
        hidden_down = jnp.take(hidden, down_row, axis=2).astype(jnp.float32)
        down_part = jnp.einsum('ptkc,khc->ptkh', down_cot, down_blk.astype(jnp.float32))
        grad_hidden = jnp.einsum('ptkh,kr->ptrh', down_part, one_hot(down_row, HB, down_live), precision=highest)
        down_grad = weight_term(jnp.einsum('ptkh,ptkc->pkhc', hidden_down, down_cot), grad_scale, down_live)
        grad_gate = (grad_hidden * up_val * sigmoid_gate * (1.0 + gate_val * (1.0 - sigmoid_gate))).astype(jnp.bfloat16)
        grad_up = (grad_hidden * active).astype(jnp.bfloat16)
        gate_back = jnp.take(grad_gate, gate_row, axis=2).astype(jnp.float32)
        up_back = jnp.take(grad_up, up_row, axis=2).astype(jnp.float32)
        gate_grad = weight_term(jnp.einsum('ptkc,ptkh->pkch', gate_in, gate_back), grad_scale, gate_live)
        up_grad = weight_term(jnp.einsum('ptkc,ptkh->pkch', up_in, up_back), grad_scale, up_live)
        back_gate = jnp.einsum('ptkh,kch->ptkc', gate_back, gate_blk.astype(jnp.float32))
        back_up = jnp.einsum('ptkh,kch->ptkc', up_back, up_blk.astype(jnp.float32))
        partial_sum = jnp.einsum('ptkc,kd->ptdc', back_gate, one_hot(gate_feat, DB, gate_live), precision=highest)
        partial_sum = partial_sum + jnp.einsum('ptkc,kd->ptdc', back_up, one_hot(up_feat, DB, up_live), precision=highest)
        rounded_sum = lax.optimization_barrier(partial_sum.astype(jnp.bfloat16))
        return (running + rounded_sum.astype(jnp.float32), (gate_grad, up_grad, down_grad))
    start_sum = jnp.zeros((N_DP, TOK, DB, BLOCK), jnp.float32)
    total, grads = lax.scan(owner, start_sum, (gate_w, up_w, down_w, gate_list, up_list, down_list))
    grad_x = total.reshape(TOKENS, D).astype(jnp.bfloat16)
    return (grad_x, grads[0], grads[1], grads[2])
```

```python
import functools
import math

import jax
import jax.numpy as jnp
from jax import lax
from jax.experimental import pallas as pl
from jax.experimental.pallas import tpu as pltpu
from jax.sharding import PartitionSpec as P

BF = jnp.bfloat16
F32 = jnp.float32
NB = 128
HB = 4
DB = 32
NS = 24
NT = 32
NP = 16
UNROLL = 8


def dot(a, b, ca, cb):
    return lax.dot_general(a, b, (((ca,), (cb,)), ((), ())), preferred_element_type=F32)


def slots(body):
    def some(i, carry):
        for u in range(UNROLL):
            body(i * UNROLL + u)
        return carry

    lax.fori_loop(0, NS // UNROLL, some, 0)


def feature(e):
    return lax.shift_right_logical(jnp.maximum(e, 0), 2)


def row(e):
    return jnp.maximum(e, 0) & (HB - 1)


def place(e, z, core):
    d = feature(e)
    rel = (lax.shift_right_logical(d, 1) - z) & 15
    group = (d & 1) ^ core
    lane = rel & 3
    step = lax.shift_right_logical(rel, 2)
    step = jnp.where(lane == 3, (step + 1) & 3, step)
    return jnp.where(e >= 0, group * 16 + lane * 4 + step, DB)


def forward_kernel(gl, ul, dl, here, acts, gw, uw, dw, p_own, p_other, gg_ref, gu_ref, hid_ref, prods, acc, accp):
    z, core = here[0], here[1]
    acc[...] = jnp.zeros_like(acc)
    accp[...] = jnp.zeros_like(accp)

    def project(which, entries, side, weights, contract):
        def multiply(k):
            prods[k] = dot(acts[feature(entries[0, k]), side], weights[0, k], 1, contract)

        def add(k):
            e = entries[0, k]
            r = jnp.where(e >= 0, row(e), HB)
            acc[which, r] += prods[k]

        slots(multiply)
        slots(add)

    project(0, gl, 0, gw, 0)
    project(1, ul, 0, uw, 0)
    project(2, dl, 1, dw, 1)
    for r in range(HB):
        gate, up, gh = acc[0, r], acc[1, r], acc[2, r]
        sig = jax.nn.sigmoid(gate)
        act = gate * sig
        hid_ref[r] = (act * up).astype(BF)
        gg_ref[r] = (gh * up * sig * (1.0 + gate * (1.0 - sig))).astype(BF)
        gu_ref[r] = (gh * act).astype(BF)

    def back(entries, grads, weights):
        def multiply(k):
            prods[k] = dot(grads[row(entries[0, k])], weights[0, k], 1, 1)

        def add(k):
            accp[place(entries[0, k], z, core)] += prods[k]

        slots(multiply)
        slots(add)

    back(gl, gg_ref, gw)
    back(ul, gu_ref, uw)
    for i in range(16):
        p_own[i] = accp[i].astype(BF)
        p_other[i] = accp[16 + i].astype(BF)


def terms_kernel(gl, ul, dl, acts, gg, gu, hid, out, *, scale):
    def write(slot, e, product):
        live = jnp.where(e >= 0, scale, 0.0)
        out[:, slot] = (product * live).astype(BF).reshape(NP, NB // NP, NB)

    def gate(k):
        e = gl[0, k]
        write(k, e, dot(acts[feature(e), 0], gg[row(e)], 0, 0))

    def up(k):
        e = ul[0, k]
        write(NS + k, e, dot(acts[feature(e), 0], gu[row(e)], 0, 0))

    def down(k):
        e = dl[0, k]
        write(2 * NS + k, e, dot(hid[row(e)], acts[feature(e), 1], 0, 0))

    slots(gate)
    slots(up)
    slots(down)


SMEM = pl.BlockSpec(memory_space=pltpu.SMEM)
VMEM = pl.BlockSpec(memory_space=pltpu.VMEM)


def forward(lists, here, acts, weights):
    block = jax.ShapeDtypeStruct((HB, NB, NB), BF)
    half = jax.ShapeDtypeStruct((16, NB, NB), BF)
    return pl.pallas_call(
        forward_kernel,
        in_specs=[SMEM] * 4 + [VMEM] * 4,
        out_specs=[VMEM] * 5,
        out_shape=[half, half, block, block, block],
        scratch_shapes=[
            pltpu.VMEM((NS, NB, NB), F32),
            pltpu.VMEM((3, HB + 1, NB, NB), F32),
            pltpu.VMEM((DB + 1, NB, NB), F32),
        ],
        compiler_params=pltpu.CompilerParams(vmem_limit_bytes=24 << 20),
        name="forward_backward",
    )(*lists, here, acts, *weights)


def weight_terms(lists, acts, gg, gu, hid, scale):
    return pl.pallas_call(
        functools.partial(terms_kernel, scale=scale),
        in_specs=[SMEM] * 3 + [VMEM] * 4,
        out_specs=VMEM,
        out_shape=jax.ShapeDtypeStruct((NP, 3 * NS, NB // NP, NB), BF),
        compiler_params=pltpu.CompilerParams(vmem_limit_bytes=16 << 20),
        name="weight_terms",
    )(*lists, acts, gg, gu, hid)


def shift(x, steps):
    return lax.ppermute(x, "tensor", [(i, (i + 2 * steps) % NT) for i in range(NT)])


def swap(x):
    return lax.ppermute(x, "tensor", [(i, i ^ 1) for i in range(NT)])


def total(*parts):
    return functools.reduce(jnp.add, [p.astype(F32) for p in parts]).astype(BF)


def reduce_features(p_own, p_other):
    s = total(p_own, swap(p_other)).reshape(4, 4, NB, NB)
    from_left = shift(s[1], 1)
    from_right = shift(s[3], -1)
    from_left2 = shift(s[2, :2], 2)
    from_right2 = shift(s[2, 2:], -2)
    u = [
        total(s[0, 0], from_left[0], from_right[0], from_left2[0], from_right2[1]),
        total(s[0, 1], from_left[1], from_right[1], from_left2[1]),
        total(s[0, 2], from_left[2], from_right[2]),
        total(s[0, 3], from_left[3], from_right[3], from_right2[0]),
    ]
    return total(u[0], shift(u[1], 4), shift(u[2], 8), shift(u[3], -4))


def on_device(inputs, cotangent, gate_w, up_w, down_w, gate_list, up_list, down_list):
    scale = 1.0 / math.sqrt(inputs.shape[0] * NP)
    me = lax.axis_index("tensor")
    here = jnp.stack([me // 2, me % 2]).astype(jnp.int32)
    lists = (gate_list, up_list, down_list)
    acts = lax.all_gather(jnp.stack([inputs, cotangent]), "tensor", axis=0)
    p_own, p_other, gg, gu, hid = forward(lists, here, acts, (gate_w, up_w, down_w))
    terms = weight_terms(lists, acts, gg, gu, hid, scale)
    got = lax.all_to_all(terms, "dp", 0, 0, tiled=True)
    grad_x = reduce_features(p_own, p_other)
    grads = jnp.sum(got.astype(F32), axis=0).astype(BF)
    return grad_x, grads[None, :NS], grads[None, NS : 2 * NS], grads[None, 2 * NS :]


def solution(mesh):
    w4, l2 = P("tensor", None, None, None), P("tensor", None)
    scattered = P("tensor", None, "dp", None)
    return jax.shard_map(
        on_device,
        mesh=mesh,
        in_specs=(P("dp", "tensor"), P("dp", "tensor"), w4, w4, w4, l2, l2, l2),
        out_specs=(P("dp", "tensor"), scattered, scattered, scattered),
        check_vma=False,
    )
```

```python
import functools
import math

import jax
import jax.numpy as jnp
from jax import lax
from jax.experimental import pallas as pl
from jax.experimental.pallas import tpu as pltpu
from jax.sharding import PartitionSpec as P


BF = jnp.bfloat16
F32 = jnp.float32
NB = 128
HB = 4
DB = 32
NS = 24
NT = 32
NP = 16
UNROLL = 24
NZ = 16
FAR = (0, 5, -5)
NEAR = (1, 2)
OPPOSITE = 8


def dot(a, b, ca, cb):
    return lax.dot_general(a, b, (((ca,), (cb,)), ((), ())), preferred_element_type=F32)


def slots(body):
    def some(i, carry):
        for u in range(UNROLL):
            body(i * UNROLL + u)
        return carry

    lax.fori_loop(0, NS // UNROLL, some, 0)


def feature(e):
    return lax.shift_right_logical(jnp.maximum(e, 0), 2)


def row(e):
    return jnp.maximum(e, 0) & (HB - 1)


def orders(core):
    held, sent = {}, {}
    for other in range(2):
        for f, far in enumerate(FAR):
            held[other * NZ + far % NZ] = other * 3 + f
            sent[other * NZ + far % NZ] = other * 16 + 12 + f
            for n, near in enumerate(NEAR):
                for way in (1, -1):
                    at = other * NZ + (way * near + far) % NZ
                    mine = (way == 1) == (core == 0)
                    held[at] = 19 + n * 6 + (1 - other) * 3 + f if mine else 6 + n * 6 + other * 3 + f
                    sent[at] = n * 6 + other * 3 + f if mine else 16 + n * 6 + (1 - other) * 3 + f
        held[other * NZ + OPPOSITE] = 31 if other else 18
        sent[other * NZ + OPPOSITE] = 31 if other else 15
    for table in (held, sent):
        assert sorted(table) == sorted(table.values()) == list(range(2 * NZ))
    return [held[i] for i in range(2 * NZ)] + [sent[i] for i in range(2 * NZ)]


def place(e, here, table):
    d = feature(e)
    offset = (lax.shift_right_logical(d, 1) - here[0]) & (NZ - 1)
    return here[2 + table * 2 * NZ + ((d & 1) ^ here[1]) * NZ + offset]


def forward_kernel(gl, ul, dl, here, far, far_s, near, near_s, gw, uw, dw, p_own, p_other, gg_ref, gu_ref, hid_ref, acts, acc, accp, weights, sems):
    loads = []
    for src, start, size in (
        (far, 0, 3),
        (far_s, 3, 3),
        (near, 6, 13),
        (near_s, 19, 13),
    ):
        loads.append(pltpu.make_async_copy(src, acts.at[pl.ds(start, size)], sems.at[len(loads)]))
    for src, dst in (
        (gw.at[0], weights.at[0]),
        (uw.at[0], weights.at[1]),
        (dw.at[0], weights.at[2]),
    ):
        loads.append(pltpu.make_async_copy(src, dst, sems.at[len(loads)]))
    for load in loads:
        load.start()
    acc[...] = jnp.zeros_like(acc)
    accp[...] = jnp.zeros_like(accp)
    for load in loads[:4]:
        load.wait()

    def project(which, entries, side, contract):
        loads[4 + which].wait()

        def add(k):
            e = entries[0, k]
            r = jnp.where(e >= 0, row(e), HB)
            acc[which, r] += dot(acts[place(e, here, 0), side], weights[which, k], 1, contract)

        slots(add)

    project(0, gl, 0, 0)
    project(1, ul, 0, 0)
    project(2, dl, 1, 1)
    for r in range(HB):
        gate, up, gh = acc[0, r], acc[1, r], acc[2, r]
        sig = jax.nn.sigmoid(gate)
        act = gate * sig
        hid_ref[r] = (act * up).astype(BF)
        gg_ref[r] = (gh * up * sig * (1.0 + gate * (1.0 - sig))).astype(BF)
        gu_ref[r] = (gh * act).astype(BF)

    def back(entries, grads, which):
        def add(k):
            e = entries[0, k]
            accp[jnp.where(e >= 0, place(e, here, 1), DB)] += dot(grads[row(e)], weights[which, k], 1, 1)

        slots(add)

    back(gl, gg_ref, 0)
    back(ul, gu_ref, 1)
    for i in range(16):
        p_own[i] = accp[i].astype(BF)
        p_other[i] = accp[16 + i].astype(BF)


def terms_kernel(gl, ul, dl, here, acts, gg, gu, hid, out, *, scale):
    def write(slot, e, product):
        live = jnp.where(e >= 0, scale, 0.0)
        out[:, slot] = (product * live).astype(BF).reshape(NP, NB // NP, NB)

    def gate(k):
        e = gl[0, k]
        write(k, e, dot(acts[place(e, here, 0), 0], gg[row(e)], 0, 0))

    def up(k):
        e = ul[0, k]
        write(NS + k, e, dot(acts[place(e, here, 0), 0], gu[row(e)], 0, 0))

    def down(k):
        e = dl[0, k]
        write(2 * NS + k, e, dot(hid[row(e)], acts[place(e, here, 0), 1], 0, 0))

    slots(gate)
    slots(up)
    slots(down)


SMEM = pl.BlockSpec(memory_space=pltpu.SMEM)
VMEM = pl.BlockSpec(memory_space=pltpu.VMEM)
ANY = pl.BlockSpec(memory_space=pl.ANY)
HBM = pl.BlockSpec(memory_space=pltpu.HBM)


def forward(lists, here, acts, weights):
    block = jax.ShapeDtypeStruct((HB, NB, NB), BF)
    half = jax.ShapeDtypeStruct((16, NB, NB), BF)
    return pl.pallas_call(
        forward_kernel,
        in_specs=[SMEM] * 4 + [ANY] * 4 + [HBM] * 3,
        out_specs=[VMEM] * 6,
        out_shape=[half, half, block, block, block, jax.ShapeDtypeStruct((DB, 2, NB, NB), BF)],
        scratch_shapes=[
            pltpu.VMEM((3, HB + 1, NB, NB), F32),
            pltpu.VMEM((DB + 1, NB, NB), F32),
            pltpu.VMEM((3, NS, NB, NB), BF),
            pltpu.SemaphoreType.DMA((7,)),
        ],
        compiler_params=pltpu.CompilerParams(vmem_limit_bytes=44 << 20),
        name="forward_backward",
    )(*lists, here, *acts, *weights)


def weight_terms(lists, here, acts, gg, gu, hid, scale):
    return pl.pallas_call(
        functools.partial(terms_kernel, scale=scale),
        in_specs=[SMEM] * 4 + [VMEM] * 4,
        out_specs=VMEM,
        out_shape=jax.ShapeDtypeStruct((NP, 3 * NS, NB // NP, NB), BF),
        compiler_params=pltpu.CompilerParams(vmem_limit_bytes=6 << 20),
        name="weight_terms",
    )(*lists, here, acts, gg, gu, hid)


def shift(x, steps):
    return lax.ppermute(x, "tensor", [(i, (i + 2 * steps) % NT) for i in range(NT)])


def swap(x):
    return lax.ppermute(x, "tensor", [(i, i ^ 1) for i in range(NT)])


def total(*parts):
    return functools.reduce(jnp.add, [p.astype(F32) for p in parts]).astype(BF)


def part_ways(x, steps):
    return lax.ppermute(x, "tensor", [(i, (i + (2 * steps if i % 2 == 0 else -2 * steps)) % NT) for i in range(NT)])


def reduce_features(p_own, p_other):
    p_other = swap(p_other)
    s = total(p_own, p_other)
    r1 = part_ways(s[:6], NEAR[0])
    r2 = part_ways(s[6:12], NEAR[1])
    r3 = shift(s[15], OPPOSITE - FAR[1])
    t = [total(s[12], r1[0], r2[0]), total(s[13], r1[1], r2[1], r3), total(s[14], r1[2], r2[2])]
    t_other = swap(total(r1[3:], r2[3:]))
    u = [total(t[f], t_other[f]) for f in range(3)]
    return total(u[0], shift(u[1], FAR[1]), shift(u[2], FAR[2]))


def gather_features(x):
    far = jnp.stack([x, shift(x, -FAR[1]), shift(x, -FAR[2])])
    far_s = swap(far)
    full = jnp.concatenate([far, far_s])
    one = part_ways(full, NEAR[0])
    two = part_ways(full, NEAR[1])
    last = shift(far[1], FAR[1] - OPPOSITE)[None]
    near = jnp.concatenate([one, two, last])
    return far, far_s, near, swap(near)


def on_device(inputs, cotangent, gate_w, up_w, down_w, gate_list, up_list, down_list):
    scale = 1.0 / math.sqrt(inputs.shape[0] * NP)
    me = lax.axis_index("tensor")
    tables = jnp.array([orders(0), orders(1)], jnp.int32)
    here = jnp.concatenate([jnp.stack([me // 2, me % 2]).astype(jnp.int32), tables[me % 2]])
    lists = (gate_list, up_list, down_list)
    pieces = gather_features(jnp.stack([inputs, cotangent]))
    p_own, p_other, gg, gu, hid, acts = forward(lists, here, pieces, [pltpu.with_memory_space_constraint(w, pltpu.HBM) for w in (gate_w, up_w, down_w)])
    terms = weight_terms(lists, here, acts, gg, gu, hid, scale)
    got = lax.all_to_all(terms, "dp", 0, 0, tiled=True)
    grad_x = reduce_features(p_own, p_other)
    grads = jnp.sum(got.astype(F32), axis=0).astype(BF)
    return grad_x, grads[None, :NS], grads[None, NS : 2 * NS], grads[None, 2 * NS :]


def solution(mesh):
    w4, l2 = P("tensor", None, None, None), P("tensor", None)
    scattered = P("tensor", None, "dp", None)
    return jax.shard_map(
        on_device,
        mesh=mesh,
        in_specs=(P("dp", "tensor"), P("dp", "tensor"), w4, w4, w4, l2, l2, l2),
        out_specs=(P("dp", "tensor"), scattered, scattered, scattered),
        check_vma=False,
    )
```

```python
import functools
import math

import jax
import jax.numpy as jnp
from jax import lax
from jax.experimental import pallas as pl
from jax.experimental.pallas import tpu as pltpu
from jax.sharding import PartitionSpec as P


BF = jnp.bfloat16
F32 = jnp.float32
NB = 128
HB = 4
DB = 32
NS = 24
NT = 32
NP = 16
UNROLL = 24
SUM_SLOTS = 12
NZ = 16
NZ = 16


def dot(a, b, ca, cb):
    return lax.dot_general(a, b, (((ca,), (cb,)), ((), ())), preferred_element_type=F32)


def slots(body):
    def some(i, carry):
        for u in range(UNROLL):
            body(i * UNROLL + u)
        return carry

    lax.fori_loop(0, NS // UNROLL, some, 0)


def feature(e):
    return lax.shift_right_logical(jnp.maximum(e, 0), 2)


def row(e):
    return jnp.maximum(e, 0) & (HB - 1)


def orders(core):
    way = 1 - 2 * core
    behind, ahead = [0, -4 * way, 8, 4 * way], [0, 4 * way, 8, -4 * way]
    held = [(0, o) for o in behind] + [(1, o) for o in ahead]
    held += [(0, o - way) for o in behind] + [(1, o - way) for o in ahead]
    held += [(0, -2 * way), (0, -6 * way), (1, -2 * way), (1, -6 * way)]
    held += [(1, o + way) for o in ahead] + [(0, o + way) for o in behind]
    held += [(1, 2 * way), (1, 6 * way), (0, 2 * way), (0, 6 * way)]
    sent = [(0, o + way) for o in ahead] + [(1, o + way) for o in ahead]
    sent += [(0, 2 * way), (0, 6 * way), (1, 2 * way), (1, 6 * way)]
    sent += [(0, o) for o in ahead]
    sent += [(1, o - way) for o in behind] + [(0, o - way) for o in behind]
    sent += [(1, -2 * way), (1, -6 * way), (0, -2 * way), (0, -6 * way)]
    sent += [(1, o) for o in behind]
    tables = []
    for blocks in (held, sent):
        at = {other * NZ + offset % NZ: i for i, (other, offset) in enumerate(blocks)}
        assert sorted(at) == list(range(2 * NZ))
        tables += [at[i] for i in range(2 * NZ)]
    return tables


def place(e, here, table):
    d = feature(e)
    offset = (lax.shift_right_logical(d, 1) - here[0]) & (NZ - 1)
    return here[2 + table * 2 * NZ + ((d & 1) ^ here[1]) * NZ + offset]


def forward_kernel(gl, ul, dl, here, far, far_s, one, two, one_s, two_s, gw, uw, dw, p_own, p_other, gg_ref, gu_ref, hid_ref, acts, acc, accp, weights, sems):
    loads = []
    for src, start, size in (
        (far, 0, 4),
        (far_s, 4, 4),
        (one, 8, 8),
        (two, 16, 4),
        (one_s, 20, 8),
        (two_s, 28, 4),
    ):
        loads.append(pltpu.make_async_copy(src, acts.at[pl.ds(start, size)], sems.at[len(loads)]))
    for src, dst in (
        (gw.at[0], weights.at[0]),
        (uw.at[0], weights.at[1]),
        (dw.at[0], weights.at[2]),
    ):
        loads.append(pltpu.make_async_copy(src, dst, sems.at[len(loads)]))
    for load in loads:
        load.start()
    acc[...] = jnp.zeros_like(acc)
    accp[...] = jnp.zeros_like(accp)
    for load in loads[:6]:
        load.wait()

    def project(which, entries, side, contract):
        loads[6 + which].wait()

        def add(k):
            e = entries[0, k]
            r = jnp.where(e >= 0, row(e), HB)
            acc[which, r] += dot(acts[place(e, here, 0), side], weights[which, k], 1, contract)

        slots(add)

    project(0, gl, 0, 0)
    project(1, ul, 0, 0)
    project(2, dl, 1, 1)
    for r in range(HB):
        gate, up, gh = acc[0, r], acc[1, r], acc[2, r]
        sig = jax.nn.sigmoid(gate)
        act = gate * sig
        hid_ref[r] = (act * up).astype(BF)
        gg_ref[r] = (gh * up * sig * (1.0 + gate * (1.0 - sig))).astype(BF)
        gu_ref[r] = (gh * act).astype(BF)

    def back(entries, grads, which):
        def add(k):
            e = entries[0, k]
            accp[jnp.where(e >= 0, place(e, here, 1), DB)] += dot(grads[row(e)], weights[which, k], 1, 1)

        slots(add)

    back(gl, gg_ref, 0)
    back(ul, gu_ref, 1)
    for i in range(16):
        p_own[i] = accp[i].astype(BF)
        p_other[i] = accp[16 + i].astype(BF)


def terms_kernel(gl, ul, dl, here, acts, gg, gu, hid, out, *, scale):
    def write(slot, e, product):
        live = jnp.where(e >= 0, scale, 0.0)
        out[:, slot] = (product * live).astype(BF).reshape(NP, NB // NP, NB)

    def gate(k):
        e = gl[0, k]
        write(k, e, dot(acts[place(e, here, 0), 0], gg[row(e)], 0, 0))

    def up(k):
        e = ul[0, k]
        write(NS + k, e, dot(acts[place(e, here, 0), 0], gu[row(e)], 0, 0))

    def down(k):
        e = dl[0, k]
        write(2 * NS + k, e, dot(hid[row(e)], acts[place(e, here, 0), 1], 0, 0))

    slots(gate)
    slots(up)
    slots(down)


def sum_kernel(got, gate, up, down, held, sems):
    loads = []
    for i in range(3 * NS // SUM_SLOTS):
        part = pl.ds(i * SUM_SLOTS, SUM_SLOTS)
        loads.append(pltpu.make_async_copy(got.at[:, part], held.at[:, part], sems.at[i]))
        loads[-1].start()
    for i, load in enumerate(loads):
        load.wait()
        part = pl.ds(i * SUM_SLOTS, SUM_SLOTS)
        acc = held[0, part].astype(F32)
        for p in range(1, NP):
            acc += held[p, part].astype(F32)
        out = (gate, up, down)[i * SUM_SLOTS // NS]
        out[pl.ds(i * SUM_SLOTS % NS, SUM_SLOTS)] = acc.astype(BF)


SMEM = pl.BlockSpec(memory_space=pltpu.SMEM)
VMEM = pl.BlockSpec(memory_space=pltpu.VMEM)
ANY = pl.BlockSpec(memory_space=pl.ANY)
HBM = pl.BlockSpec(memory_space=pltpu.HBM)


def forward(lists, here, acts, weights):
    block = jax.ShapeDtypeStruct((HB, NB, NB), BF)
    half = jax.ShapeDtypeStruct((16, NB, NB), BF)
    return pl.pallas_call(
        forward_kernel,
        in_specs=[SMEM] * 4 + [ANY] * 6 + [HBM] * 3,
        out_specs=[VMEM] * 6,
        out_shape=[half, half, block, block, block, jax.ShapeDtypeStruct((DB, 2, NB, NB), BF)],
        scratch_shapes=[
            pltpu.VMEM((3, HB + 1, NB, NB), F32),
            pltpu.VMEM((DB + 1, NB, NB), F32),
            pltpu.VMEM((3, NS, NB, NB), BF),
            pltpu.SemaphoreType.DMA((9,)),
        ],
        compiler_params=pltpu.CompilerParams(vmem_limit_bytes=16 << 20),
        name="forward_backward",
    )(*lists, here, *acts, *weights)


def weight_terms(lists, here, acts, gg, gu, hid, scale):
    return pl.pallas_call(
        functools.partial(terms_kernel, scale=scale),
        in_specs=[SMEM] * 4 + [VMEM] * 4,
        out_specs=VMEM,
        out_shape=jax.ShapeDtypeStruct((NP, 3 * NS, NB // NP, NB), BF),
        compiler_params=pltpu.CompilerParams(vmem_limit_bytes=6 << 20),
        name="weight_terms",
    )(*lists, here, acts, gg, gu, hid)


def sum_groups(got):
    rows = jax.ShapeDtypeStruct((NS, NB // NP, NB), BF)
    return pl.pallas_call(
        sum_kernel,
        in_specs=[ANY],
        out_specs=[VMEM] * 3,
        out_shape=[rows] * 3,
        scratch_shapes=[
            pltpu.VMEM((NP, 3 * NS, NB // NP, NB), BF),
            pltpu.SemaphoreType.DMA((3 * NS // SUM_SLOTS,)),
        ],
        compiler_params=pltpu.CompilerParams(vmem_limit_bytes=8 << 20),
        name="sum_groups",
    )(got)


def shift(x, steps):
    return lax.ppermute(x, "tensor", [(i, (i + 2 * steps) % NT) for i in range(NT)])


def swap(x):
    return lax.ppermute(x, "tensor", [(i, i ^ 1) for i in range(NT)])


def total(*parts):
    return functools.reduce(jnp.add, [p.astype(F32) for p in parts]).astype(BF)


def part_ways(x, steps):
    return lax.ppermute(x, "tensor", [(i, (i + (2 * steps if i % 2 == 0 else -2 * steps)) % NT) for i in range(NT)])


def reduce_features(p_own, p_other):
    p_other = swap(p_other)
    s = total(p_own, p_other)
    r1 = part_ways(s[:8], 1)
    r2 = part_ways(s[8:12], 2)
    own = [total(s[12 + i], r1[i], *([r2[i]] if i < 2 else [])) for i in range(4)]
    other = [total(r1[4 + i], *([r2[2 + i]] if i < 2 else [])) for i in range(4)]
    got = swap(jnp.stack([own[3], other[3], other[0], other[2]]))
    r4 = part_ways(jnp.stack([total(own[1], got[1]), total(other[1], got[0])]), 4)
    r8 = shift(total(own[2], got[3]), 8)
    last = swap(r4[1])
    return total(own[0], got[2], r8, r4[0], last)


def gather_features(x):
    opposite = shift(x, 8)
    back = part_ways(x, 4)
    forth = part_ways(x, -4)
    far = jnp.stack([x, back, opposite, forth])
    far_s = swap(far)
    one = part_ways(jnp.concatenate([far, far_s]), 1)
    two = part_ways(jnp.concatenate([far[:2], far_s[:1], far_s[3:]]), 2)
    one_s = swap(one)
    return far, far_s, one, two, one_s, swap(two)


def on_device(inputs, cotangent, gate_w, up_w, down_w, gate_list, up_list, down_list):
    scale = 1.0 / math.sqrt(inputs.shape[0] * NP)
    me = lax.axis_index("tensor")
    tables = jnp.array([orders(0), orders(1)], jnp.int32)
    here = jnp.concatenate([jnp.stack([me // 2, me % 2]).astype(jnp.int32), tables[me % 2]])
    lists = (gate_list, up_list, down_list)
    pieces = gather_features(jnp.stack([inputs, cotangent]))
    p_own, p_other, gg, gu, hid, acts = forward(lists, here, pieces, [pltpu.with_memory_space_constraint(w, pltpu.HBM) for w in (gate_w, up_w, down_w)])
    terms = weight_terms(lists, here, acts, gg, gu, hid, scale)
    got = lax.all_to_all(terms, "dp", 0, 0, tiled=True)
    grad_x = reduce_features(p_own, p_other)
    return grad_x, *(g[None] for g in sum_groups(got))


def solution(mesh):
    w4, l2 = P("tensor", None, None, None), P("tensor", None)
    scattered = P("tensor", None, "dp", None)
    return jax.shard_map(
        on_device,
        mesh=mesh,
        in_specs=(P("dp", "tensor"), P("dp", "tensor"), w4, w4, w4, l2, l2, l2),
        out_specs=(P("dp", "tensor"), scattered, scattered, scattered),
        check_vma=False,
    )
```

```python
import functools
import math

import jax
import jax.numpy as jnp
from jax import lax
from jax.experimental import pallas as pl
from jax.experimental.pallas import tpu as pltpu
from jax.sharding import PartitionSpec as P


BF = jnp.bfloat16
F32 = jnp.float32
NB = 128
HB = 4
DB = 32
NS = 24
NT = 32
NP = 16
UNROLL = 24
SUM_SLOTS = 12
NZ = 16
NZ = 16


def dot(a, b, ca, cb):
    return lax.dot_general(a, b, (((ca,), (cb,)), ((), ())), preferred_element_type=F32)


def slots(body):
    def some(i, carry):
        for u in range(UNROLL):
            body(i * UNROLL + u)
        return carry

    lax.fori_loop(0, NS // UNROLL, some, 0)


def feature(e):
    return lax.shift_right_logical(jnp.maximum(e, 0), 2)


def row(e):
    return jnp.maximum(e, 0) & (HB - 1)


def orders(core):
    way = 1 - 2 * core
    behind, ahead = [0, -4 * way, 8, 4 * way], [0, 4 * way, 8, -4 * way]
    held = [(0, o) for o in behind] + [(1, o) for o in ahead]
    held += [(0, o - way) for o in behind] + [(1, o - way) for o in ahead]
    held += [(0, -2 * way), (0, -6 * way), (1, -2 * way), (1, -6 * way)]
    held += [(1, o + way) for o in ahead] + [(0, o + way) for o in behind]
    held += [(1, 2 * way), (1, 6 * way), (0, 2 * way), (0, 6 * way)]
    sent = [(0, o + way) for o in ahead] + [(1, o + way) for o in ahead]
    sent += [(0, 2 * way), (0, 6 * way), (1, 2 * way), (1, 6 * way)]
    sent += [(0, o) for o in ahead]
    sent += [(1, o - way) for o in behind] + [(0, o - way) for o in behind]
    sent += [(1, -2 * way), (1, -6 * way), (0, -2 * way), (0, -6 * way)]
    sent += [(1, o) for o in behind]
    tables = []
    for blocks in (held, sent):
        at = {other * NZ + offset % NZ: i for i, (other, offset) in enumerate(blocks)}
        assert sorted(at) == list(range(2 * NZ))
        tables += [at[i] for i in range(2 * NZ)]
    return tables


def place(e, here, table):
    d = feature(e)
    offset = (lax.shift_right_logical(d, 1) - here[0]) & (NZ - 1)
    return here[2 + table * 2 * NZ + ((d & 1) ^ here[1]) * NZ + offset]


def forward_kernel(gl, ul, dl, here, far, far_s, one, two, one_s, two_s, gw, uw, dw, p_own, p_other, gg_ref, gu_ref, hid_ref, acts, acc, accp, weights, sems):
    loads = []
    for src, start, size in (
        (far, 0, 4),
        (far_s, 4, 4),
        (one, 8, 8),
        (two, 16, 4),
        (one_s, 20, 8),
        (two_s, 28, 4),
    ):
        loads.append(pltpu.make_async_copy(src, acts.at[pl.ds(start, size)], sems.at[len(loads)]))
    for src, dst in (
        (gw.at[0], weights.at[0]),
        (uw.at[0], weights.at[1]),
        (dw.at[0], weights.at[2]),
    ):
        loads.append(pltpu.make_async_copy(src, dst, sems.at[len(loads)]))
    for load in loads:
        load.start()
    acc[...] = jnp.zeros_like(acc)
    accp[...] = jnp.zeros_like(accp)
    for load in loads[:6]:
        load.wait()

    def project(which, entries, side, contract):
        loads[6 + which].wait()

        def add(k):
            e = entries[0, k]
            r = jnp.where(e >= 0, row(e), HB)
            acc[which, r] += dot(acts[place(e, here, 0), side], weights[which, k], 1, contract)

        slots(add)

    project(0, gl, 0, 0)
    project(1, ul, 0, 0)
    project(2, dl, 1, 1)
    for r in range(HB):
        gate, up, gh = acc[0, r], acc[1, r], acc[2, r]
        sig = jax.nn.sigmoid(gate)
        act = gate * sig
        hid_ref[r] = (act * up).astype(BF)
        gg_ref[r] = (gh * up * sig * (1.0 + gate * (1.0 - sig))).astype(BF)
        gu_ref[r] = (gh * act).astype(BF)

    def back(entries, grads, which):
        def add(k):
            e = entries[0, k]
            accp[jnp.where(e >= 0, place(e, here, 1), DB)] += dot(grads[row(e)], weights[which, k], 1, 1)

        slots(add)

    back(gl, gg_ref, 0)
    back(ul, gu_ref, 1)
    for i in range(16):
        p_own[i] = accp[i].astype(BF)
        p_other[i] = accp[16 + i].astype(BF)


def terms_kernel(gl, ul, dl, here, acts, gg, gu, hid, out, held, sems, *, scale):
    def write(slot, e, product):
        live = jnp.where(e >= 0, scale, 0.0)
        held[:, slot] = (product * live).astype(BF).reshape(NP, NB // NP, NB)

    def gate(k):
        e = gl[0, k]
        write(k, e, dot(acts[place(e, here, 0), 0], gg[row(e)], 0, 0))

    def up(k):
        e = ul[0, k]
        write(NS + k, e, dot(acts[place(e, here, 0), 0], gu[row(e)], 0, 0))

    def down(k):
        e = dl[0, k]
        write(2 * NS + k, e, dot(hid[row(e)], acts[place(e, here, 0), 1], 0, 0))

    stores = []
    for i, project in enumerate((gate, up, down)):
        slots(project)
        part = pl.ds(i * NS, NS)
        stores.append(pltpu.make_async_copy(held.at[:, part], out.at[:, part], sems.at[i]))
        stores[-1].start()
    for store in stores:
        store.wait()


def sum_kernel(got, gate, up, down, held, sems):
    loads = []
    for i in range(3 * NS // SUM_SLOTS):
        part = pl.ds(i * SUM_SLOTS, SUM_SLOTS)
        loads.append(pltpu.make_async_copy(got.at[:, part], held.at[:, part], sems.at[i]))
        loads[-1].start()
    for i, load in enumerate(loads):
        load.wait()
        part = pl.ds(i * SUM_SLOTS, SUM_SLOTS)
        acc = held[0, part].astype(F32)
        for p in range(1, NP):
            acc += held[p, part].astype(F32)
        out = (gate, up, down)[i * SUM_SLOTS // NS]
        out[pl.ds(i * SUM_SLOTS % NS, SUM_SLOTS)] = acc.astype(BF)


SMEM = pl.BlockSpec(memory_space=pltpu.SMEM)
VMEM = pl.BlockSpec(memory_space=pltpu.VMEM)
ANY = pl.BlockSpec(memory_space=pl.ANY)
HBM = pl.BlockSpec(memory_space=pltpu.HBM)


def forward(lists, here, acts, weights):
    block = jax.ShapeDtypeStruct((HB, NB, NB), BF)
    half = jax.ShapeDtypeStruct((16, NB, NB), BF)
    return pl.pallas_call(
        forward_kernel,
        in_specs=[SMEM] * 4 + [ANY] * 6 + [HBM] * 3,
        out_specs=[VMEM] * 6,
        out_shape=[half, half, block, block, block, jax.ShapeDtypeStruct((DB, 2, NB, NB), BF)],
        scratch_shapes=[
            pltpu.VMEM((3, HB + 1, NB, NB), F32),
            pltpu.VMEM((DB + 1, NB, NB), F32),
            pltpu.VMEM((3, NS, NB, NB), BF),
            pltpu.SemaphoreType.DMA((9,)),
        ],
        compiler_params=pltpu.CompilerParams(vmem_limit_bytes=16 << 20),
        name="forward_backward",
    )(*lists, here, *acts, *weights)


def weight_terms(lists, here, acts, gg, gu, hid, scale):
    return pl.pallas_call(
        functools.partial(terms_kernel, scale=scale),
        in_specs=[SMEM] * 4 + [VMEM] * 4,
        out_specs=HBM,
        out_shape=pltpu.HBM((NP, 3 * NS, NB // NP, NB), BF),
        scratch_shapes=[
            pltpu.VMEM((NP, 3 * NS, NB // NP, NB), BF),
            pltpu.SemaphoreType.DMA((3,)),
        ],
        compiler_params=pltpu.CompilerParams(vmem_limit_bytes=6 << 20),
        name="weight_terms",
    )(*lists, here, acts, gg, gu, hid)


def sum_groups(got):
    rows = jax.ShapeDtypeStruct((NS, NB // NP, NB), BF)
    return pl.pallas_call(
        sum_kernel,
        in_specs=[ANY],
        out_specs=[VMEM] * 3,
        out_shape=[rows] * 3,
        scratch_shapes=[
            pltpu.VMEM((NP, 3 * NS, NB // NP, NB), BF),
            pltpu.SemaphoreType.DMA((3 * NS // SUM_SLOTS,)),
        ],
        compiler_params=pltpu.CompilerParams(vmem_limit_bytes=8 << 20),
        name="sum_groups",
    )(got)


def shift(x, steps):
    return lax.ppermute(x, "tensor", [(i, (i + 2 * steps) % NT) for i in range(NT)])


def swap(x):
    return lax.ppermute(x, "tensor", [(i, i ^ 1) for i in range(NT)])


def total(*parts):
    return functools.reduce(jnp.add, [p.astype(F32) for p in parts]).astype(BF)


def part_ways(x, steps):
    return lax.ppermute(x, "tensor", [(i, (i + (2 * steps if i % 2 == 0 else -2 * steps)) % NT) for i in range(NT)])


def reduce_features(p_own, p_other):
    p_other = swap(p_other)
    s = total(p_own, p_other)
    r1 = part_ways(s[:8], 1)
    r2 = part_ways(s[8:12], 2)
    own = [total(s[12 + i], r1[i], *([r2[i]] if i < 2 else [])) for i in range(4)]
    other = [total(r1[4 + i], *([r2[2 + i]] if i < 2 else [])) for i in range(4)]
    got = swap(jnp.stack([own[3], other[3], other[0], other[2]]))
    r4 = part_ways(jnp.stack([total(own[1], got[1]), total(other[1], got[0])]), 4)
    r8 = shift(total(own[2], got[3]), 8)
    last = swap(r4[1])
    return total(own[0], got[2], r8, r4[0], last)


def gather_features(x):
    opposite = shift(x, 8)
    back = part_ways(x, 4)
    forth = part_ways(x, -4)
    far = jnp.stack([x, back, opposite, forth])
    far_s = swap(far)
    one = part_ways(jnp.concatenate([far, far_s]), 1)
    two = part_ways(jnp.concatenate([far[:2], far_s[:1], far_s[3:]]), 2)
    one_s = swap(one)
    return far, far_s, one, two, one_s, swap(two)


def on_device(inputs, cotangent, gate_w, up_w, down_w, gate_list, up_list, down_list):
    scale = 1.0 / math.sqrt(inputs.shape[0] * NP)
    me = lax.axis_index("tensor")
    tables = jnp.array([orders(0), orders(1)], jnp.int32)
    here = jnp.concatenate([jnp.stack([me // 2, me % 2]).astype(jnp.int32), tables[me % 2]])
    lists = (gate_list, up_list, down_list)
    pieces = gather_features(jnp.stack([inputs, cotangent]))
    p_own, p_other, gg, gu, hid, acts = forward(lists, here, pieces, [pltpu.with_memory_space_constraint(w, pltpu.HBM) for w in (gate_w, up_w, down_w)])
    terms = weight_terms(lists, here, acts, gg, gu, hid, scale)
    got = lax.all_to_all(terms, "dp", 0, 0, tiled=True)
    grad_x = reduce_features(p_own, p_other)
    return grad_x, *(g[None] for g in sum_groups(got))


def solution(mesh):
    w4, l2 = P("tensor", None, None, None), P("tensor", None)
    scattered = P("tensor", None, "dp", None)
    return jax.shard_map(
        on_device,
        mesh=mesh,
        in_specs=(P("dp", "tensor"), P("dp", "tensor"), w4, w4, w4, l2, l2, l2),
        out_specs=(P("dp", "tensor"), scattered, scattered, scattered),
        check_vma=False,
    )
```

```python
import functools
import math

import jax
import jax.numpy as jnp
from jax import lax
from jax.experimental import pallas as pl
from jax.experimental.pallas import tpu as pltpu
from jax.sharding import PartitionSpec as P


BF = jnp.bfloat16
F32 = jnp.float32
NB = 128
HB = 4
DB = 32
NS = 24
NT = 32
NP = 16
UNROLL = 24
SUM_SLOTS = 12
NZ = 16
NZ = 16


def dot(a, b, ca, cb):
    return lax.dot_general(a, b, (((ca,), (cb,)), ((), ())), preferred_element_type=F32)


def slots(body):
    def some(i, carry):
        for u in range(UNROLL):
            body(i * UNROLL + u)
        return carry

    lax.fori_loop(0, NS // UNROLL, some, 0)


def feature(e):
    return lax.shift_right_logical(jnp.maximum(e, 0), 2)


def row(e):
    return jnp.maximum(e, 0) & (HB - 1)


def orders(core):
    way = 1 - 2 * core
    behind, ahead = [0, -4 * way, 8, 4 * way], [0, 4 * way, 8, -4 * way]
    held = [(0, o) for o in behind] + [(1, o) for o in ahead]
    held += [(0, o - way) for o in behind] + [(1, o - way) for o in ahead]
    held += [(0, -2 * way), (0, -6 * way), (1, -2 * way), (1, -6 * way)]
    held += [(1, o + way) for o in ahead] + [(0, o + way) for o in behind]
    held += [(1, 2 * way), (1, 6 * way), (0, 2 * way), (0, 6 * way)]
    sent = [(0, o + way) for o in ahead] + [(1, o + way) for o in ahead]
    sent += [(0, 2 * way), (0, 6 * way), (1, 2 * way), (1, 6 * way)]
    sent += [(0, o) for o in ahead]
    sent += [(1, o - way) for o in behind] + [(0, o - way) for o in behind]
    sent += [(1, -2 * way), (1, -6 * way), (0, -2 * way), (0, -6 * way)]
    sent += [(1, o) for o in behind]
    tables = []
    for blocks in (held, sent):
        at = {other * NZ + offset % NZ: i for i, (other, offset) in enumerate(blocks)}
        assert sorted(at) == list(range(2 * NZ))
        tables += [at[i] for i in range(2 * NZ)]
    return tables


def place(e, here, table):
    d = feature(e)
    offset = (lax.shift_right_logical(d, 1) - here[0]) & (NZ - 1)
    return here[2 + table * 2 * NZ + ((d & 1) ^ here[1]) * NZ + offset]


def forward_kernel(gl, ul, dl, here, far, far_s, one, two, one_s, two_s, gw, uw, dw, p_own, p_other, gg_ref, gu_ref, hid_ref, acts, acc, accp, weights, sems):
    pieces = ((far, 0, 4), (far_s, 4, 4), (one, 8, 8), (two, 16, 4), (one_s, 20, 8), (two_s, 28, 4))

    def bring(i, side):
        src, start, size = pieces[i]
        return pltpu.make_async_copy(src.at[:, side], acts.at[pl.ds(start, size), side], sems.at[6 * side + i])

    sides = [[bring(i, side) for i in range(6)] for side in range(2)]
    heavy = [pltpu.make_async_copy(w.at[0], weights.at[i], sems.at[12 + i]) for i, w in enumerate((gw, uw, dw))]
    for load in (heavy[0], *sides[0], heavy[1], *sides[1], heavy[2]):
        load.start()
    acc[...] = jnp.zeros_like(acc)
    accp[...] = jnp.zeros_like(accp)
    for load in sides[0]:
        load.wait()

    def project(which, entries, side, contract):
        heavy[which].wait()

        def add(k):
            e = entries[0, k]
            r = jnp.where(e >= 0, row(e), HB)
            acc[which, r] += dot(acts[place(e, here, 0), side], weights[which, k], 1, contract)

        slots(add)

    project(0, gl, 0, 0)
    project(1, ul, 0, 0)
    for load in sides[1]:
        load.wait()
    project(2, dl, 1, 1)
    for r in range(HB):
        gate, up, gh = acc[0, r], acc[1, r], acc[2, r]
        sig = jax.nn.sigmoid(gate)
        act = gate * sig
        hid_ref[r] = (act * up).astype(BF)
        gg_ref[r] = (gh * up * sig * (1.0 + gate * (1.0 - sig))).astype(BF)
        gu_ref[r] = (gh * act).astype(BF)

    def back(entries, grads, which):
        def add(k):
            e = entries[0, k]
            accp[jnp.where(e >= 0, place(e, here, 1), DB)] += dot(grads[row(e)], weights[which, k], 1, 1)

        slots(add)

    back(gl, gg_ref, 0)
    back(ul, gu_ref, 1)
    for i in range(16):
        p_own[i] = accp[i].astype(BF)
        p_other[i] = accp[16 + i].astype(BF)


def terms_kernel(gl, ul, dl, here, acts, gg, gu, hid, out, held, sems, *, scale):
    def write(slot, e, product):
        live = jnp.where(e >= 0, scale, 0.0)
        held[:, slot] = (product * live).astype(BF).reshape(NP, NB // NP, NB)

    def gate(k):
        e = gl[0, k]
        write(k, e, dot(acts[place(e, here, 0), 0], gg[row(e)], 0, 0))

    def up(k):
        e = ul[0, k]
        write(NS + k, e, dot(acts[place(e, here, 0), 0], gu[row(e)], 0, 0))

    def down(k):
        e = dl[0, k]
        write(2 * NS + k, e, dot(hid[row(e)], acts[place(e, here, 0), 1], 0, 0))

    stores = []
    for i, project in enumerate((gate, up, down)):
        slots(project)
        part = pl.ds(i * NS, NS)
        stores.append(pltpu.make_async_copy(held.at[:, part], out.at[:, part], sems.at[i]))
        stores[-1].start()
    for store in stores:
        store.wait()


def sum_kernel(got, gate, up, down, held, sems):
    loads = []
    for i in range(3 * NS // SUM_SLOTS):
        part = pl.ds(i * SUM_SLOTS, SUM_SLOTS)
        loads.append(pltpu.make_async_copy(got.at[:, part], held.at[:, part], sems.at[i]))
        loads[-1].start()
    for i, load in enumerate(loads):
        load.wait()
        part = pl.ds(i * SUM_SLOTS, SUM_SLOTS)
        acc = held[0, part].astype(F32)
        for p in range(1, NP):
            acc += held[p, part].astype(F32)
        out = (gate, up, down)[i * SUM_SLOTS // NS]
        out[pl.ds(i * SUM_SLOTS % NS, SUM_SLOTS)] = acc.astype(BF)


SMEM = pl.BlockSpec(memory_space=pltpu.SMEM)
VMEM = pl.BlockSpec(memory_space=pltpu.VMEM)
ANY = pl.BlockSpec(memory_space=pl.ANY)
HBM = pl.BlockSpec(memory_space=pltpu.HBM)


def forward(lists, here, acts, weights):
    block = jax.ShapeDtypeStruct((HB, NB, NB), BF)
    half = jax.ShapeDtypeStruct((16, NB, NB), BF)
    return pl.pallas_call(
        forward_kernel,
        in_specs=[SMEM] * 4 + [ANY] * 6 + [HBM] * 3,
        out_specs=[VMEM] * 6,
        out_shape=[half, half, block, block, block, jax.ShapeDtypeStruct((DB, 2, NB, NB), BF)],
        scratch_shapes=[
            pltpu.VMEM((3, HB + 1, NB, NB), F32),
            pltpu.VMEM((DB + 1, NB, NB), F32),
            pltpu.VMEM((3, NS, NB, NB), BF),
            pltpu.SemaphoreType.DMA((15,)),
        ],
        compiler_params=pltpu.CompilerParams(vmem_limit_bytes=16 << 20),
        name="forward_backward",
    )(*lists, here, *acts, *weights)


def weight_terms(lists, here, acts, gg, gu, hid, scale):
    return pl.pallas_call(
        functools.partial(terms_kernel, scale=scale),
        in_specs=[SMEM] * 4 + [VMEM] * 4,
        out_specs=HBM,
        out_shape=pltpu.HBM((NP, 3 * NS, NB // NP, NB), BF),
        scratch_shapes=[
            pltpu.VMEM((NP, 3 * NS, NB // NP, NB), BF),
            pltpu.SemaphoreType.DMA((3,)),
        ],
        compiler_params=pltpu.CompilerParams(vmem_limit_bytes=6 << 20),
        name="weight_terms",
    )(*lists, here, acts, gg, gu, hid)


def sum_groups(got):
    rows = jax.ShapeDtypeStruct((NS, NB // NP, NB), BF)
    return pl.pallas_call(
        sum_kernel,
        in_specs=[ANY],
        out_specs=[VMEM] * 3,
        out_shape=[rows] * 3,
        scratch_shapes=[
            pltpu.VMEM((NP, 3 * NS, NB // NP, NB), BF),
            pltpu.SemaphoreType.DMA((3 * NS // SUM_SLOTS,)),
        ],
        compiler_params=pltpu.CompilerParams(vmem_limit_bytes=8 << 20),
        name="sum_groups",
    )(got)


def shift(x, steps):
    return lax.ppermute(x, "tensor", [(i, (i + 2 * steps) % NT) for i in range(NT)])


def swap(x):
    return lax.ppermute(x, "tensor", [(i, i ^ 1) for i in range(NT)])


def total(*parts):
    return functools.reduce(jnp.add, [p.astype(F32) for p in parts]).astype(BF)


def part_ways(x, steps):
    return lax.ppermute(x, "tensor", [(i, (i + (2 * steps if i % 2 == 0 else -2 * steps)) % NT) for i in range(NT)])


def reduce_features(p_own, p_other):
    p_other = swap(p_other)
    s = total(p_own, p_other)
    r1 = part_ways(s[:8], 1)
    r2 = part_ways(s[8:12], 2)
    own = [total(s[12 + i], r1[i], *([r2[i]] if i < 2 else [])) for i in range(4)]
    other = [total(r1[4 + i], *([r2[2 + i]] if i < 2 else [])) for i in range(4)]
    got = swap(jnp.stack([own[3], other[3], other[0], other[2]]))
    r4 = part_ways(jnp.stack([total(own[1], got[1]), total(other[1], got[0])]), 4)
    r8 = shift(total(own[2], got[3]), 8)
    last = swap(r4[1])
    return total(own[0], got[2], r8, r4[0], last)


def gather_features(x):
    opposite = shift(x, 8)
    back = part_ways(x, 4)
    forth = part_ways(x, -4)
    far = jnp.stack([x, back, opposite, forth])
    far_s = swap(far)
    one = part_ways(jnp.concatenate([far, far_s]), 1)
    two = part_ways(jnp.concatenate([far[:2], far_s[:1], far_s[3:]]), 2)
    one_s = swap(one)
    return far, far_s, one, two, one_s, swap(two)


def on_device(inputs, cotangent, gate_w, up_w, down_w, gate_list, up_list, down_list):
    scale = 1.0 / math.sqrt(inputs.shape[0] * NP)
    me = lax.axis_index("tensor")
    tables = jnp.array([orders(0), orders(1)], jnp.int32)
    here = jnp.concatenate([jnp.stack([me // 2, me % 2]).astype(jnp.int32), tables[me % 2]])
    lists = (gate_list, up_list, down_list)
    pieces = gather_features(jnp.stack([inputs, cotangent]))
    p_own, p_other, gg, gu, hid, acts = forward(lists, here, pieces, [pltpu.with_memory_space_constraint(w, pltpu.HBM) for w in (gate_w, up_w, down_w)])
    terms = weight_terms(lists, here, acts, gg, gu, hid, scale)
    got = lax.all_to_all(terms, "dp", 0, 0, tiled=True)
    grad_x = reduce_features(p_own, p_other)
    return grad_x, *(g[None] for g in sum_groups(got))


def solution(mesh):
    w4, l2 = P("tensor", None, None, None), P("tensor", None)
    scattered = P("tensor", None, "dp", None)
    return jax.shard_map(
        on_device,
        mesh=mesh,
        in_specs=(P("dp", "tensor"), P("dp", "tensor"), w4, w4, w4, l2, l2, l2),
        out_specs=(P("dp", "tensor"), scattered, scattered, scattered),
        check_vma=False,
    )
```
